32 devices in a mesh: groups: 2 (over y), seq: 4 (over z), mp: 4 (over x, core).
Axes of the slice: x: 2, y: 2, z: 4, core: 2. Of those that a mesh axis runs over, the one named last changes fastest.
Arguments:
- points: bfloat16 [131072, 256], P(('groups', 'seq'), 'mp'), parts along dimension 0, may hold values from -6 to 6
- w_query: bfloat16 [256, 256], replicated, may hold values from -2 to 2
- w_key: bfloat16 [256, 256], replicated, may hold values from -2 to 2
- w_value: bfloat16 [256, 256], replicated, may hold values from -0.375 to 0.375
- w_out: bfloat16 [256, 256], replicated, may hold values from -0.375 to 0.375
- w_up: bfloat16 [256, 1024], replicated, may hold values from -0.375 to 0.375
- w_down: bfloat16 [1024, 256], replicated, may hold values from -0.1875 to 0.1875
- w_pool: bfloat16 [2048, 512], replicated, may hold values from -0.125 to 0.125
- keep_count: int32 [32], P(('groups', 'seq', 'mp')), parts along dimension 0, may hold values from 0 to 32, as said below
Outputs:
- refined: bfloat16 [131072, 256], P(('groups', 'seq', 'mp')), parts along dimension 0
- coarse: bfloat16 [32768, 512], P(('groups', 'seq', 'mp')), parts along dimension 0
The draws below stay inside these ranges and needn't reach their ends.
There are 2 independent parts, one for each index of `groups`. The reference program is written for one: setup_inputs(seed, part) draws one part's arguments, and reference() takes and returns one part's arrays. A program takes and returns all parts, laid end to end along the dimension named above; an argument that names none is the same for every part. Nothing has to cross between parts.
Inputs may be any that keep to these rules, and one draw needn't show every extreme that they name: `keep_count`: in every draw some block keeps 0 tiles and some block keeps all 32.
All inputs are finite; a program needn't handle non-finite values.
Results may differ from the reference program's by a relative error of at most 0.0061.
Values may be sent and summed in bfloat16 or wider, within the bound.
No kernel may reach another device: no remote copies, remote signals or barrier semaphores. Data moves between devices by JAX's collectives and lax.ppermute only.
A program may use at most 192 MiB of HBM per device.

```python
import math
import jax
import jax.numpy as jnp
from jax import lax

WIDTH = 256
HEADS = 8
FFN_WIDTH = 1024
POOL_WIDTH = 512
WINDOW = 32
DILATION = 4
TILE_PARENTS = 16
POINTS_DEV = 16384
POINTS = 65536
TILES_DEV = 32
N_SEQ = 4
N_MP = 4


def weight_pair(key):
    common = jnp.clip(jax.random.normal(jax.random.fold_in(key, 11), (WIDTH, WIDTH), jnp.float32), -4.0, 4.0)
    second = jnp.clip(jax.random.normal(jax.random.fold_in(key, 12), (WIDTH, WIDTH), jnp.float32), -4.0, 4.0)
    factor = 1.0 / math.sqrt(WIDTH)
    return (factor * common, factor * second)


def draw_w_query(key, part):
    return weight_pair(key)[0].astype(jnp.bfloat16)


def draw_w_key(key, part):
    return weight_pair(key)[1].astype(jnp.bfloat16)


def draw_keep_count(key, part):
    owners = N_SEQ * N_MP
    counts = jax.random.randint(jax.random.fold_in(key, 21), (owners,), 0, TILES_DEV + 1)
    first_owner = jax.random.randint(jax.random.fold_in(key, 22), (), 0, owners)
    places = jnp.arange(owners)
    counts = jnp.where(places == first_owner, 0, counts)
    counts = jnp.where(places == (first_owner + 1) % owners, TILES_DEV, counts)
    return counts.astype(jnp.int32)


def levels(own_key, extent, pieces, low, largest):
    def one(position, blocks):
        heights = jax.random.uniform(jax.random.fold_in(jax.random.fold_in(own_key, 6), position), (blocks,), jnp.float32, low / len(pieces), largest / len(pieces))
        return jnp.repeat(jnp.exp(heights), extent[position] // blocks).reshape((-1,) + (1,) * (len(extent) - position - 1))

    loudness = one(*pieces[0])
    for cut in pieces[1:]:
        loudness = loudness * one(*cut)
    return loudness


def gaussian(key, extent, width, limit, cuts=(), held_as=jnp.bfloat16):
    result = width * jax.random.normal(key, extent, jnp.float32)
    if cuts:
        result = result * levels(key, extent, cuts, -0.22, 0.18)
    return jnp.clip(result, -limit, limit).astype(held_as)


def setup_inputs(seed: int = 0, part: int = 0) -> dict:
    seeds = jax.random.split(jax.random.key(seed), 10)
    part_splits = jax.random.split(jax.random.fold_in(seeds[9], part), 10)
    return {
        "points": gaussian(part_splits[0], (POINTS, WIDTH), 1.0, 6.0, ((0, 4), (1, 4))),
        "w_query": draw_w_query(jax.random.fold_in(seeds[9], 71), part),
        "w_key": draw_w_key(jax.random.fold_in(seeds[9], 71), part),
        "w_value": gaussian(seeds[3], (WIDTH, WIDTH), WIDTH ** -0.5, 0.375),
        "w_out": gaussian(seeds[4], (WIDTH, WIDTH), WIDTH ** -0.5, 0.375),
        "w_up": gaussian(seeds[5], (WIDTH, FFN_WIDTH), WIDTH ** -0.5, 0.375),
        "w_down": gaussian(seeds[6], (FFN_WIDTH, WIDTH), FFN_WIDTH ** -0.5, 0.1875),
        "w_pool": gaussian(seeds[7], (8 * WIDTH, POOL_WIDTH), (8 * WIDTH) ** -0.5, 0.125),
        "keep_count": draw_keep_count(jax.random.fold_in(jax.random.fold_in(seeds[9], part), 71), part),
    }


def norm_rows(values):
    centre = values - lax.optimization_barrier(jnp.mean(values, axis=-1, keepdims=True))
    spread = lax.optimization_barrier(jnp.mean(centre * centre, axis=-1, keepdims=True))
    return centre * lax.rsqrt(spread + 1e-05)

def project(normed, weight):
    return jnp.dot(normed, weight, preferred_element_type=jnp.float32).astype(jnp.bfloat16)

def attend_exact(queries, key_rows, value_rows):
    row_count = queries.shape[0]
    head_size = WIDTH // HEADS
    window_count = row_count // (WINDOW * DILATION)
    layout = (window_count, WINDOW, DILATION, HEADS, head_size)
    scores = jnp.einsum('wjrhd,wkrhd->wrhjk', queries.reshape(layout).astype(jnp.float32), key_rows.reshape(layout).astype(jnp.float32)) / math.sqrt(head_size)
    highest = lax.optimization_barrier(jnp.max(scores, axis=-1, keepdims=True))
    weights = jnp.exp(scores - highest)
    weight_bf = (weights / lax.optimization_barrier(jnp.sum(weights, axis=-1, keepdims=True))).astype(jnp.bfloat16)
    mixed_rows = jnp.einsum('wrhjk,wkrhd->wjrhd', weight_bf.astype(jnp.float32), value_rows.reshape(layout).astype(jnp.float32))
    return mixed_rows.reshape(row_count, WIDTH).astype(jnp.bfloat16)

def reference(points, w_query, w_key, w_value, w_out, w_up, w_down, w_pool, keep_count):
    normed = norm_rows(points.astype(jnp.float32)).astype(jnp.bfloat16)
    queries = project(normed, w_query)
    key_rows = project(normed, w_key)
    value_rows = project(normed, w_value)
    margin = WINDOW * DILATION // 2
    rolled = tuple((jnp.roll(matrix, -margin, axis=0).reshape(N_SEQ, POINTS_DEV, WIDTH) for matrix in (queries, key_rows, value_rows)))
    attended = lax.map(lambda triple: attend_exact(triple[0], triple[1], triple[2]), rolled)
    attended = jnp.roll(attended.reshape(POINTS, WIDTH), margin, axis=0)

    def finish(block_pair):
        hidden_sum = block_pair[0].astype(jnp.float32) + jnp.dot(block_pair[1], w_out, preferred_element_type=jnp.float32)
        normed_two = norm_rows(hidden_sum).astype(jnp.bfloat16)
        activated = jax.nn.gelu(jnp.dot(normed_two, w_up, preferred_element_type=jnp.float32)).astype(jnp.bfloat16)
        return (hidden_sum + jnp.dot(activated, w_down, preferred_element_type=jnp.float32)).astype(jnp.bfloat16)
    refined = lax.map(finish, (points.reshape(N_SEQ, POINTS_DEV, WIDTH), attended.reshape(N_SEQ, POINTS_DEV, WIDTH)))
    refined = refined.reshape(POINTS, WIDTH)
    pooled = jnp.dot(refined.reshape(POINTS // 8, 8 * WIDTH), w_pool, preferred_element_type=jnp.float32).astype(jnp.bfloat16)
    owners = N_SEQ * N_MP
    tiles = pooled.reshape(owners, TILES_DEV, TILE_PARENTS, POOL_WIDTH)
    before = jnp.roll(tiles, 1, axis=0)
    kept = keep_count.astype(jnp.int32)[:, None]
    kept_before = jnp.roll(keep_count.astype(jnp.int32), 1)[:, None]
    slots = jnp.arange(2 * TILES_DEV, dtype=jnp.int32)[None, :]
    own_index = jnp.broadcast_to(jnp.clip(slots, 0, TILES_DEV - 1), (owners, 2 * TILES_DEV)).astype(jnp.int32)
    came_index = jnp.clip(slots - kept + kept_before, 0, TILES_DEV - 1).astype(jnp.int32)
    own_take = jnp.take_along_axis(tiles, own_index[:, :, None, None], axis=1)
    came_take = jnp.take_along_axis(before, came_index[:, :, None, None], axis=1)
    use_own = (slots < kept)[:, :, None, None]
    use_came = ((slots >= kept) & (slots - kept < TILES_DEV - kept_before))[:, :, None, None]
    coarse = jnp.where(use_own, own_take, jnp.where(use_came, came_take, jnp.zeros_like(own_take)))
    return (refined, coarse.reshape(owners * 2 * TILES_DEV * TILE_PARENTS, POOL_WIDTH))
```

```python
import functools
import math

import jax
import jax.numpy as jnp
import numpy as np
from jax import lax
from jax.experimental import pallas as pl
from jax.experimental.pallas import tpu as pltpu
from jax.sharding import PartitionSpec as P

HEADS = 8
WINDOW = 32
DILATION = 4
TILE_PARENTS = 16
CHILDREN = 8
BLOCK = WINDOW * DILATION
HALF = BLOCK // 2
STEP = 3
CHUNK_STEPS = (3, 3, 3, 2)

BF = jnp.bfloat16
F32 = jnp.float32


def gather_order():
    place = np.zeros((BLOCK, 2 * BLOCK), np.float32)
    for r in range(DILATION):
        for j in range(WINDOW):
            place[r * WINDOW + j, HALF + DILATION * j + r] = 1.0
    return place


def output_order():
    back = np.zeros((2 * BLOCK, BLOCK), np.float32)
    for r in range(DILATION):
        for j in range(WINDOW):
            p = DILATION * j + r
            back[p, r * WINDOW + j] = 1.0
            back[BLOCK + (p % CHILDREN) * TILE_PARENTS + p // CHILDREN, r * WINDOW + j] = 1.0
    return back


def head_masks(width):
    size = width // HEADS
    half = WINDOW // 2
    rows = np.arange(HEADS * half)[:, None] // half
    cols = np.arange(width)[None, :] // size
    mask = (rows == cols).astype(np.float32)
    return np.concatenate([mask, mask], axis=0)


def norm_rows(values):
    centre = values - jnp.mean(values, axis=-1, keepdims=True)
    spread = jnp.mean(centre * centre, axis=-1, keepdims=True)
    return centre * lax.rsqrt(spread + 1e-05)


def dot_nn(a, b):
    return lax.dot_general(a, b, (((1,), (0,)), ((), ())), preferred_element_type=F32)


def dot_nt(a, b):
    return lax.dot_general(a, b, (((1,), (1,)), ((), ())), preferred_element_type=F32)


def segment_max(scores):
    width = scores.shape[1] // 2
    run = WINDOW // 2
    top = jnp.maximum(scores[:, :width], scores[:, width:])
    for shift in (1, 2, 4, 8):
        top = jnp.maximum(top, pltpu.roll(top, shift, 1))
    lane = lax.broadcasted_iota(jnp.int32, top.shape, 1)
    top = jnp.where(lane % run == run - 1, top, -jnp.inf)
    for shift in (1, 2, 4, 8):
        top = jnp.maximum(top, pltpu.roll(top, width - shift, 1))
    return top


def layer_step(x, w, win_count):
    width = x.shape[1]
    normed = norm_rows(x).astype(BF)
    qkv = dot_nn(normed, w["qkv"][...]).astype(BF)
    mask = w["mask"][...]
    run = WINDOW // 2
    groups = win_count * DILATION
    scores = []
    for g in range(groups):
        rows = slice(g * WINDOW, (g + 1) * WINDOW)
        q = qkv[rows, :width]
        k = qkv[rows, width : 2 * width]
        wide = jnp.concatenate([k[:run]] * HEADS + [k[run:]] * HEADS, axis=0) * mask
        scores.append(dot_nt(q, wide))
    scores = jnp.concatenate(scores, axis=0)
    top = segment_max(scores)
    top = jnp.concatenate([top, top], axis=1)
    factor = math.log2(math.e) / math.sqrt(width // HEADS)
    weights = jnp.exp2((scores - top) * factor).astype(BF)
    total = dot_nn(weights, mask)
    mixed = []
    for g in range(groups):
        rows = slice(g * WINDOW, (g + 1) * WINDOW)
        v = qkv[rows, 2 * width :]
        wide = jnp.concatenate([v[:run]] * HEADS + [v[run:]] * HEADS, axis=0) * mask
        mixed.append(dot_nn(weights[rows], wide))
    attended = (jnp.concatenate(mixed, axis=0) / total).astype(BF)
    hidden = x + dot_nn(attended, w["out"][...])
    normed_two = norm_rows(hidden).astype(BF)
    up = dot_nn(normed_two, w["up"][...])
    inner = up * (0.7978845608028654 + 0.035677408136300125 * (up * up))
    activated = (0.5 * up * (1.0 + jnp.tanh(inner))).astype(BF)
    return (hidden + dot_nn(activated, w["down"][...])).astype(BF)


def chunk_kernel(spec, *refs):
    first_tile, tiles, first_window, steps, last, aliased, quarter, feat = spec
    names = ["place", "own"]
    n_recv = 3
    it = iter(refs)
    place_ref = next(it)
    own = next(it)
    recv = [next(it) for _ in range(n_recv)]
    if first_window > 1:
        before = [next(it) for _ in range(n_recv)]
    if last:
        halo_own = next(it)
        start = [next(it) for _ in range(n_recv)]
    hbm = {k: next(it) for k in ("gather", "mask", "qkv", "out", "up", "down", "back", "pool")}
    if aliased:
        next(it)
    refined, pooled = next(it), next(it)
    xbuf, ybuf, pbuf = next(it), next(it), next(it)
    w = {k: next(it) for k in ("gather", "mask", "qkv", "out", "up", "down", "back", "pool")}
    pooled_buf = next(it)
    in_sem, w_sem, out_sem, pool_sem = next(it), next(it), next(it), next(it)
    mp_index = place_ref[0]
    copies = []

    def bring(src, source_shift, col, width):
        j = lax.rem(mp_index + 4 - source_shift, 4)
        dst = xbuf.at[pl.ds(pl.multiple_of(j * feat, feat), feat), pl.ds(col, width)]
        c = pltpu.make_async_copy(src, dst, in_sem.at[len(copies)])
        c.start()
        copies.append(c)

    def own_cols(tile, count):
        return own.at[:, pl.ds(pl.multiple_of(mp_index * quarter + tile * BLOCK, BLOCK), count * BLOCK)]

    lead = 0
    if first_window > 1:
        lead = 1
        for s in range(n_recv):
            n_before = before[s].shape[1]
            bring(before[s].at[:, pl.ds(n_before - BLOCK, BLOCK)], s + 1, 0, BLOCK)
        bring(own_cols(first_tile - 1, 1), 0, 0, BLOCK)
    for s in range(n_recv):
        bring(recv[s], s + 1, lead * BLOCK, recv[s].shape[1])
    bring(own_cols(first_tile, tiles), 0, lead * BLOCK, tiles * BLOCK)
    if last:
        bring(halo_own, 0, (lead + tiles) * BLOCK, BLOCK)
        for s in range(n_recv):
            bring(start[s].at[:, pl.ds(0, BLOCK)], s + 1, (lead + tiles + 1) * BLOCK, BLOCK)
        bring(own_cols(0, 1), 0, (lead + tiles + 1) * BLOCK, BLOCK)
    loads = {}
    for n, key in enumerate(hbm):
        loads[key] = pltpu.make_async_copy(hbm[key], w[key], w_sem.at[n])
        loads[key].start()
    for c in copies:
        c.wait()
    for key in hbm:
        if key != "pool":
            loads[key].wait()

    rows_step = STEP * BLOCK
    windows = steps * STEP
    width = 4 * feat

    def step(s, carry):
        gather = w["gather"][...]
        xs = []
        for n in range(STEP):
            col = pl.multiple_of((s * STEP + n) * BLOCK, BLOCK)
            xs.append(dot_nt(gather, xbuf[:, pl.ds(col, 2 * BLOCK)]))
        ys = layer_step(jnp.concatenate(xs, axis=0), w, STEP)
        back = w["back"][...]
        for n in range(STEP):
            both = dot_nn(back, ys[n * BLOCK : (n + 1) * BLOCK]).astype(BF)
            row = pl.multiple_of((s * STEP + n) * BLOCK, BLOCK)
            ybuf[pl.ds(row, BLOCK), :] = both[:BLOCK]
            parent = pl.multiple_of((s * STEP + n) * TILE_PARENTS, TILE_PARENTS)
            for c in range(CHILDREN):
                piece = both[BLOCK + c * TILE_PARENTS : BLOCK + (c + 1) * TILE_PARENTS]
                pbuf[pl.ds(parent, TILE_PARENTS), c * width : (c + 1) * width] = piece
        return carry

    lax.fori_loop(0, steps, step, 0)
    base = first_window * BLOCK - HALF
    outs = []
    if last:
        rows = quarter - base
        outs.append(pltpu.make_async_copy(ybuf.at[pl.ds(0, rows)], refined.at[pl.ds(base, rows)], out_sem.at[0]))
        outs.append(
            pltpu.make_async_copy(
                ybuf.at[pl.ds(windows * BLOCK - HALF, HALF)], refined.at[pl.ds(0, HALF)], out_sem.at[1]
            )
        )
    else:
        rows = windows * BLOCK
        outs.append(pltpu.make_async_copy(ybuf, refined.at[pl.ds(base, rows)], out_sem.at[0]))
    for c in outs:
        c.start()
    loads["pool"].wait()
    result = dot_nn(pbuf[...], w["pool"][...])
    pooled_buf[...] = result.reshape(pooled_buf.shape).astype(BF)
    c = pltpu.make_async_copy(pooled_buf, pooled, pool_sem.at[0])
    c.start()
    c.wait()
    for c in outs:
        c.wait()


def run_chunk(spec, mp_index, own, recv, before, halo_own, start, weights, refined, rows, pool_width):
    first_tile, tiles, first_window, steps, last, aliased, quarter, feat = spec
    windows = steps * STEP
    width = 4 * feat
    args = [mp_index, own] + recv
    if first_window > 1:
        args += before
    if last:
        args += [halo_own] + start
    keys = ("gather", "mask", "qkv", "out", "up", "down", "back", "pool")
    args += [weights[k] for k in keys]
    aliases = {}
    if aliased:
        aliases = {len(args): 0}
        args.append(refined)
    any_spec = pl.BlockSpec(memory_space=pl.ANY)
    in_specs = [pl.BlockSpec(memory_space=pltpu.SMEM)] + [any_spec] * (len(args) - 1)
    halves = windows * TILE_PARENTS // 8
    scratch = [
        pltpu.VMEM((width, (windows + 1) * BLOCK), BF),
        pltpu.VMEM((windows * BLOCK, width), BF),
        pltpu.VMEM((windows * TILE_PARENTS, CHILDREN * width), BF),
    ]
    scratch += [pltpu.VMEM(weights[k].shape, BF) for k in keys]
    scratch += [
        pltpu.VMEM((halves, 8, pool_width), BF),
        pltpu.SemaphoreType.DMA((16,)),
        pltpu.SemaphoreType.DMA((len(keys),)),
        pltpu.SemaphoreType.DMA((2,)),
        pltpu.SemaphoreType.DMA((1,)),
    ]
    points = windows * BLOCK
    flops = 2 * points * (width * width * 16 + 2 * width * weights["up"].shape[1] + width * pool_width)
    return pl.pallas_call(
        functools.partial(chunk_kernel, spec),
        out_shape=(
            jax.ShapeDtypeStruct((rows, width), BF),
            jax.ShapeDtypeStruct((halves, 8, pool_width), BF),
        ),
        in_specs=in_specs,
        out_specs=(any_spec, any_spec),
        scratch_shapes=scratch,
        input_output_aliases=aliases,
        compiler_params=pltpu.CompilerParams(vmem_limit_bytes=48 << 20),
        cost_estimate=pl.CostEstimate(
            flops=flops, transcendentals=points * 1024, bytes_accessed=points * width * 4 + (4 << 20)
        ),
        name=f"layer_chunk_{first_window}",
    )(*args)


def place_kernel(counts, *refs):
    n = (len(refs) - 2) // 2
    own, came, out, zero = refs[:n], refs[n : 2 * n], refs[2 * n], refs[2 * n + 1]
    del zero
    slots = out.shape[0]
    total = slots // 2
    kept = counts[0] * 2
    kept_before = counts[1] * 2
    blank = jnp.zeros(out.shape[1:], BF)

    def clear(v, carry):
        out[v] = blank
        return carry

    lax.fori_loop(kept + total - kept_before, slots, clear, 0)
    lower = 1
    for n_piece in range(n):
        count = own[n_piece].shape[0]
        upper = min(lower + count, total)

        def keep(v, carry, piece=own[n_piece], low=lower):
            out[v] = piece[v - low]
            return carry

        def take(v, carry, piece=came[n_piece], low=lower):
            out[v + kept - kept_before] = piece[v - low]
            return carry

        lax.fori_loop(lower, jnp.minimum(kept, upper), keep, 0)
        lax.fori_loop(jnp.maximum(kept_before, lower), upper, take, 0)
        lower += count
    last = own[n - 1].shape[0] - 1

    @pl.when(kept > 0)
    def _():
        out[0] = own[n - 1][last]

    @pl.when(kept_before == 0)
    def _():
        out[kept] = came[n - 1][last]


def body(points, w_query, w_key, w_value, w_out, w_up, w_down, w_pool, keep_count):
    width = w_out.shape[0]
    feat = points.shape[1]
    ways = lax.axis_size("mp")
    seq_ways = lax.axis_size("seq")
    quarter = points.shape[0] // ways
    pool_width = w_pool.shape[1]
    mp_index = lax.axis_index("mp").astype(jnp.int32)
    own = points.T
    tiles_all = own.shape[1] // BLOCK
    tiles_quarter = quarter // BLOCK

    first = own[:, :BLOCK]
    final = own[:, own.shape[1] - BLOCK :]
    after = lax.ppermute(first, "seq", [((i + 1) % seq_ways, i) for i in range(seq_ways)])
    prior = lax.ppermute(final, "seq", [(i, (i + 1) % seq_ways) for i in range(seq_ways)])

    chunk_tiles = []
    tile = 0
    for n, steps in enumerate(CHUNK_STEPS):
        count = steps * STEP
        if n == 0:
            count += 1
        if n == len(CHUNK_STEPS) - 1:
            count = tiles_quarter - tile
        chunk_tiles.append((tile, count))
        tile += count

    head = jnp.stack([own[:, q * quarter : q * quarter + BLOCK] for q in range(1, ways)] + [after])
    tail = jnp.stack([prior] + [own[:, q * quarter - BLOCK : q * quarter] for q in range(1, ways)])
    lane = lax.broadcasted_iota(jnp.int32, (1, 1, BLOCK), 2)
    halos = jnp.where(lane < HALF, head, tail)
    halo_own = lax.dynamic_index_in_dim(halos, mp_index, 0, keepdims=False)

    received = []
    for n, (tile, count) in enumerate(chunk_tiles):
        got = []
        for s in (1, 2, 3):
            dest = (mp_index + s) % ways
            block = lax.dynamic_slice_in_dim(own, dest * quarter + tile * BLOCK, count * BLOCK, 1)
            if n == len(chunk_tiles) - 1:
                halo = lax.dynamic_index_in_dim(halos, dest, 0, keepdims=False)
                block = jnp.concatenate([block, halo], axis=1)
            got.append(lax.ppermute(block, "mp", [(i, (i + s) % ways) for i in range(ways)]))
        received.append(got)

    weights = {
        "gather": jnp.asarray(gather_order(), BF),
        "mask": jnp.asarray(head_masks(width), BF),
        "qkv": jnp.concatenate([w_query, w_key, w_value], axis=1),
        "out": w_out,
        "up": w_up,
        "down": w_down,
        "back": jnp.asarray(output_order(), BF),
        "pool": w_pool,
    }
    pairs = [(i, (i + 1) % (seq_ways * ways)) for i in range(seq_ways * ways)]
    kept_before = lax.ppermute(keep_count, ("seq", "mp"), pairs)
    refined = None
    window = 1
    own_pooled, came_pooled = [], []
    for n, steps in enumerate(CHUNK_STEPS):
        tile, count = chunk_tiles[n]
        last = n == len(CHUNK_STEPS) - 1
        spec = (tile, count, window, steps, last, n > 0, quarter, feat)
        refined, pooled = run_chunk(
            spec,
            mp_index[None],
            own,
            received[n],
            received[n - 1] if n else None,
            halo_own,
            received[0],
            weights,
            refined,
            quarter,
            pool_width,
        )
        own_pooled.append(pooled)
        came_pooled.append(lax.ppermute(pooled, ("seq", "mp"), pairs))
        window += steps * STEP

    counts = jnp.concatenate([keep_count, kept_before])
    slots = 2 * quarter // (CHILDREN * 8)
    vmem = pl.BlockSpec(memory_space=pltpu.VMEM)
    coarse = pl.pallas_call(
        place_kernel,
        out_shape=jax.ShapeDtypeStruct((slots, 8, pool_width), BF),
        in_specs=[pl.BlockSpec(memory_space=pltpu.SMEM)] + [vmem] * (2 * len(CHUNK_STEPS)),
        out_specs=vmem,
        scratch_shapes=[pltpu.VMEM((8, pool_width), BF)],
        compiler_params=pltpu.CompilerParams(vmem_limit_bytes=32 << 20),
        name="place_tiles",
    )(counts, *own_pooled, *came_pooled)
    return (refined, coarse.reshape(slots * 8, pool_width))


def solution(mesh):
    placed = (
        P(("groups", "seq"), "mp"),
        P(),
        P(),
        P(),
        P(),
        P(),
        P(),
        P(),
        P(("groups", "seq", "mp")),
    )
    return jax.shard_map(
        body,
        mesh=mesh,
        in_specs=placed,
        out_specs=(P(("groups", "seq", "mp"), None), P(("groups", "seq", "mp"), None)),
        check_vma=False,
    )
```

```python
import functools
import math

import jax
import jax.numpy as jnp
from jax import lax
from jax.experimental import pallas as pl
from jax.experimental.pallas import tpu as pltpu
from jax.sharding import PartitionSpec as P

HEADS = 8
WINDOW = 32
DILATION = 4
TILE_PARENTS = 16
CHILDREN = 8
BLOCK = WINDOW * DILATION
HALF = BLOCK // 2
CHUNKS = (7, 13, 13)
FFN_ROWS = 384
FFN_COLS = 256
SHIFTS = (3, 2, 1)

BF = jnp.bfloat16
F32 = jnp.float32


def gather_order():
    row = lax.broadcasted_iota(jnp.int32, (BLOCK, 2 * BLOCK), 0)
    col = lax.broadcasted_iota(jnp.int32, (BLOCK, 2 * BLOCK), 1)
    return (col == HALF + DILATION * (row % WINDOW) + row // WINDOW).astype(F32).astype(BF)


def output_order():
    row = lax.broadcasted_iota(jnp.int32, (2 * BLOCK, BLOCK), 0)
    col = lax.broadcasted_iota(jnp.int32, (2 * BLOCK, BLOCK), 1)
    point = DILATION * (col % WINDOW) + col // WINDOW
    by_child = BLOCK + (point % CHILDREN) * TILE_PARENTS + point // CHILDREN
    return ((row == point) | (row == by_child)).astype(F32).astype(BF)


def head_mask(width):
    rows = HEADS * WINDOW
    row = lax.broadcasted_iota(jnp.int32, (rows, width), 0)
    col = lax.broadcasted_iota(jnp.int32, (rows, width), 1)
    return (row // (WINDOW // 2) % HEADS == col // (width // HEADS)).astype(F32).astype(BF)


def norm_rows(values):
    centre = values - jnp.mean(values, axis=-1, keepdims=True)
    spread = jnp.mean(centre * centre, axis=-1, keepdims=True)
    return centre * lax.rsqrt(spread + 1e-05)


def dot_nn(a, b):
    return lax.dot_general(a, b, (((1,), (0,)), ((), ())), preferred_element_type=F32)


def dot_nt(a, b):
    return lax.dot_general(a, b, (((1,), (1,)), ((), ())), preferred_element_type=F32)


def segment_max(scores):
    width = scores.shape[1] // 2
    run = WINDOW // 2
    top = jnp.maximum(scores[:, :width], scores[:, width:])
    for shift in (1, 2, 4, 8):
        top = jnp.maximum(top, pltpu.roll(top, shift, 1))
    lane = lax.broadcasted_iota(jnp.int32, top.shape, 1)
    top = jnp.where(lane % run == run - 1, top, -jnp.inf)
    for shift in (1, 2, 4, 8):
        top = jnp.maximum(top, pltpu.roll(top, width - shift, 1))
    return top


def feed_forward(hidden, normed, up_ref, down_ref):
    hidden_width = up_ref.shape[1]
    rows = hidden.shape[0]
    done = []
    for r in range(0, rows, FFN_ROWS):
        part = slice(r, min(r + FFN_ROWS, rows))
        total = hidden[part]
        for c in range(0, hidden_width, FFN_COLS):
            up = dot_nn(normed[part], up_ref[:, c : c + FFN_COLS])
            inner = up * (0.7978845608028654 + 0.035677408136300125 * (up * up))
            half = 0.5 * up
            activated = (half + half * jnp.tanh(inner)).astype(BF)
            total = total + dot_nn(activated, down_ref[c : c + FFN_COLS, :])
        done.append(total.astype(BF))
    return jnp.concatenate(done, axis=0)


def layer(x, weights, arrive, windows):
    wq, wk, wv, wo, wu, wd = weights
    width = x.shape[1]
    normed = norm_rows(x).astype(BF)
    arrive(0, 3)
    queries = dot_nn(normed, wq[...]).astype(BF)
    keys = dot_nn(normed, wk[...]).astype(BF)
    values = dot_nn(normed, wv[...]).astype(BF)
    mask = head_mask(width)
    run = WINDOW // 2
    groups = windows * DILATION
    scores = []
    for g in range(groups):
        rows = slice(g * WINDOW, (g + 1) * WINDOW)
        k = keys[rows]
        wide = jnp.concatenate([k[:run]] * HEADS + [k[run:]] * HEADS, axis=0) * mask
        scores.append(dot_nt(queries[rows], wide))
    scores = jnp.concatenate(scores, axis=0)
    top = segment_max(scores)
    top = jnp.concatenate([top, top], axis=1)
    factor = math.log2(math.e) / math.sqrt(width // HEADS)
    shares = jnp.exp2((scores - top) * factor).astype(BF)
    total = dot_nn(shares, mask)
    mixed = []
    for g in range(groups):
        rows = slice(g * WINDOW, (g + 1) * WINDOW)
        v = values[rows]
        wide = jnp.concatenate([v[:run]] * HEADS + [v[run:]] * HEADS, axis=0) * mask
        mixed.append(dot_nn(shares[rows], wide))
    attended = (jnp.concatenate(mixed, axis=0) / total).astype(BF)
    arrive(3, 6)
    hidden = x + dot_nn(attended, wo[...])
    return feed_forward(hidden, norm_rows(hidden).astype(BF), wu, wd)


def send_kernel(quarter, wanted, mp_ref, own, *refs):
    count = len(wanted)
    outs, bufs, sems = refs[:count], refs[count : 2 * count], refs[2 * count]
    loads, puts = [], []
    for n, (shift, tile, tiles) in enumerate(wanted):
        col = tile * BLOCK
        if shift is not None:
            col = pl.multiple_of((mp_ref[0] ^ shift) * quarter + col, BLOCK)
        loads.append(pltpu.make_async_copy(own.at[:, pl.ds(col, tiles * BLOCK)], bufs[n], sems.at[0, n]))
        puts.append(pltpu.make_async_copy(bufs[n], outs[n], sems.at[1, n]))
    for c in loads:
        c.start()
    for load, put in zip(loads, puts):
        load.wait()
        put.start()
    for c in puts:
        c.wait()


def send_blocks(mp_index, own, quarter, wanted, name):
    hbm = pl.BlockSpec(memory_space=pltpu.HBM)
    return pl.pallas_call(
        functools.partial(send_kernel, quarter, wanted),
        out_shape=tuple(jax.ShapeDtypeStruct((own.shape[0], t * BLOCK), BF) for _, _, t in wanted),
        in_specs=[pl.BlockSpec(memory_space=pltpu.SMEM), hbm],
        out_specs=(hbm,) * len(wanted),
        scratch_shapes=[pltpu.VMEM((own.shape[0], t * BLOCK), BF) for _, _, t in wanted]
        + [pltpu.SemaphoreType.DMA((2, len(wanted)))],
        name=name,
    )(mp_index, *in_hbm([own]))


def last_blocks(spec, mp_index, own, after, prior, outs, bufs, edge, halo, edge_sems, load_sems, put_sems):
    quarter, ways, tile, tiles = spec
    edges, loads = [], []
    for q in range(ways):
        head = own.at[:, pl.ds((q + 1) * quarter, BLOCK)] if q + 1 < ways else after
        tail = own.at[:, pl.ds(q * quarter - BLOCK, BLOCK)] if q else prior
        edges.append(pltpu.make_async_copy(head, edge.at[0, q], edge_sems.at[2 * q]))
        edges.append(pltpu.make_async_copy(tail, edge.at[1, q], edge_sems.at[2 * q + 1]))
    for n in range(ways - 1):
        col = pl.multiple_of((mp_index ^ SHIFTS[n]) * quarter + tile * BLOCK, BLOCK)
        dst = bufs[n].at[:, pl.ds(0, tiles * BLOCK)]
        loads.append(pltpu.make_async_copy(own.at[:, pl.ds(col, tiles * BLOCK)], dst, load_sems.at[n]))
    puts = [pltpu.make_async_copy(bufs[n], outs[n], put_sems.at[n]) for n in range(ways - 1)]
    puts.append(pltpu.make_async_copy(halo.at[mp_index], outs[ways - 1], put_sems.at[ways - 1]))

    def begin():
        for c in edges + loads:
            c.start()

    def send():
        for c in edges + loads:
            c.wait()
        lane = lax.broadcasted_iota(jnp.int32, edge.shape[1:], 2)
        halo[...] = jnp.where(lane < HALF, edge[0].astype(F32), edge[1].astype(F32)).astype(BF)
        for n in range(ways - 1):
            bufs[n][:, tiles * BLOCK :] = halo[mp_index ^ SHIFTS[n]]
        for c in puts:
            c.start()

    def end():
        for c in puts:
            c.wait()

    return begin, send, end


def chunk_kernel(spec, *refs):
    first_tile, tiles, first_window, windows, last, aliased, quarter, feat, last_span = spec
    n_recv = 3
    it = iter(refs)
    place_ref = next(it)
    kept_ref = next(it)
    own = next(it)
    recv = [next(it) for _ in range(n_recv)]
    if first_window > 1:
        before = [next(it) for _ in range(n_recv)]
    if last:
        halo_own = next(it)
        start = [next(it) for _ in range(n_recv)]
        next(it)
    if not aliased:
        after, prior = next(it), next(it)
    weights_hbm = [next(it) for _ in range(7)]
    if aliased:
        next(it)
    refined, pooled = next(it), next(it)
    if not aliased:
        block_outs = [next(it) for _ in range(n_recv + 1)]
    xbuf, ybuf, pbuf, pooled_buf = (next(it) for _ in range(4))
    weights = [next(it) for _ in range(7)]
    in_sem, w_sem, out_sem, pool_sem = (next(it) for _ in range(4))
    mp_index = place_ref[0]
    if not aliased:
        block_bufs = [next(it) for _ in range(n_recv)]
        begin, send, end = last_blocks(
            (quarter, n_recv + 1) + last_span, mp_index, own, after, prior, block_outs, block_bufs, *it
        )
    copies = []
    fetch = [pltpu.make_async_copy(weights_hbm[n], weights[n], w_sem.at[n]) for n in range(7)]

    def arrive(first, limit):
        for n in range(first, limit):
            fetch[n].wait()

    def bring(src, shift, col, width):
        j = mp_index ^ shift
        dst = xbuf.at[pl.ds(pl.multiple_of(j * feat, feat), feat), pl.ds(col, width)]
        c = pltpu.make_async_copy(src, dst, in_sem.at[len(copies)])
        c.start()
        copies.append(c)

    def own_cols(tile, count):
        return own.at[:, pl.ds(pl.multiple_of(mp_index * quarter + tile * BLOCK, BLOCK), count * BLOCK)]

    lead = 0
    if first_window > 1:
        lead = 1
        for s in range(n_recv):
            n_before = before[s].shape[1]
            bring(before[s].at[:, pl.ds(n_before - BLOCK, BLOCK)], n_recv - s, 0, BLOCK)
        bring(own_cols(first_tile - 1, 1), 0, 0, BLOCK)
    for s in range(n_recv):
        bring(recv[s], n_recv - s, lead * BLOCK, recv[s].shape[1])
    bring(own_cols(first_tile, tiles), 0, lead * BLOCK, tiles * BLOCK)
    if last:
        bring(halo_own, 0, (lead + tiles) * BLOCK, BLOCK)
        for s in range(n_recv):
            bring(start[s].at[:, pl.ds(0, BLOCK)], n_recv - s, (lead + tiles + 1) * BLOCK, BLOCK)
        bring(own_cols(0, 1), 0, (lead + tiles + 1) * BLOCK, BLOCK)
    for n in range(3):
        fetch[n].start()
    gather = gather_order()
    back = output_order()
    for c in copies:
        c.wait()
    for n in range(3, 7):
        fetch[n].start()
    if not aliased:
        begin()

    width = 4 * feat
    xs = [dot_nt(gather, xbuf[:, n * BLOCK : (n + 2) * BLOCK]) for n in range(windows)]
    ys = layer(jnp.concatenate(xs, axis=0), weights[:6], arrive, windows)
    for n in range(windows):
        both = dot_nn(back, ys[n * BLOCK : (n + 1) * BLOCK]).astype(BF)
        ybuf[n * BLOCK : (n + 1) * BLOCK, :] = both[:BLOCK]
        for c in range(CHILDREN):
            piece = both[BLOCK + c * TILE_PARENTS : BLOCK + (c + 1) * TILE_PARENTS]
            pbuf[n * TILE_PARENTS : (n + 1) * TILE_PARENTS, c * width : (c + 1) * width] = piece
    if not aliased:
        send()
    base = first_window * BLOCK - HALF
    outs = []
    if last:
        rows = quarter - base
        outs.append(pltpu.make_async_copy(ybuf.at[pl.ds(0, rows)], refined.at[pl.ds(base, rows)], out_sem.at[0]))
        outs.append(
            pltpu.make_async_copy(
                ybuf.at[pl.ds(windows * BLOCK - HALF, HALF)], refined.at[pl.ds(0, HALF)], out_sem.at[1]
            )
        )
    else:
        rows = windows * BLOCK
        outs.append(pltpu.make_async_copy(ybuf, refined.at[pl.ds(base, rows)], out_sem.at[0]))
    for c in outs:
        c.start()
    arrive(6, 7)
    result = dot_nn(pbuf[...], weights[6][...])
    halves = windows * TILE_PARENTS // 8
    pooled_buf[:halves] = result.reshape((halves,) + pooled_buf.shape[1:]).astype(BF)
    if not aliased:
        pooled_buf[halves] = jnp.full(pooled_buf.shape[1:], kept_ref[0], jnp.int32).astype(F32).astype(BF)
    c = pltpu.make_async_copy(pooled_buf, pooled, pool_sem.at[0])
    c.start()
    c.wait()
    for c in outs:
        c.wait()
    if not aliased:
        end()


def run_chunk(spec, mp_index, kept, own, recv, before, halo_own, start, tied, edges, weights, refined, rows):
    first_tile, tiles, first_window, windows, last, aliased, quarter, feat, last_span = spec
    width = 4 * feat
    pool_width = weights[6].shape[1]
    smem = pl.BlockSpec(memory_space=pltpu.SMEM)
    hbm = pl.BlockSpec(memory_space=pltpu.HBM)
    any_spec = pl.BlockSpec(memory_space=pl.ANY)
    args = [mp_index, kept] + in_hbm([own]) + recv
    if first_window > 1:
        args += before
    if last:
        args += [halo_own] + start + [tied]
    if not aliased:
        args += edges
    moved = len(args)
    args += weights
    aliases = {}
    if aliased:
        aliases = {len(args): 0}
        args.append(refined)
    halves = windows * TILE_PARENTS // 8
    points = windows * BLOCK
    flops = 2 * points * (width * width * 16 + 2 * width * weights[4].shape[1] + width * pool_width)
    piece = (halves + (not aliased), 8, pool_width)
    out_shape = [jax.ShapeDtypeStruct((rows, width), BF), jax.ShapeDtypeStruct(piece, BF)]
    out_specs = [hbm, any_spec]
    scratch = [
        pltpu.VMEM((width, (windows + 1) * BLOCK), BF),
        pltpu.VMEM((points, width), BF),
        pltpu.VMEM((windows * TILE_PARENTS, CHILDREN * width), BF),
        pltpu.VMEM(piece, BF),
    ]
    scratch += [pltpu.VMEM(w.shape, BF) for w in weights]
    scratch += [
        pltpu.SemaphoreType.DMA((16,)),
        pltpu.SemaphoreType.DMA((7,)),
        pltpu.SemaphoreType.DMA((2,)),
        pltpu.SemaphoreType.DMA((1,)),
    ]
    if not aliased:
        ways = len(recv) + 1
        wide = (feat, (last_span[1] + 1) * BLOCK)
        out_shape += [jax.ShapeDtypeStruct(wide, BF)] * len(recv) + [jax.ShapeDtypeStruct((feat, BLOCK), BF)]
        out_specs += [any_spec] * ways
        scratch += [pltpu.VMEM(wide, BF)] * len(recv)
        scratch += [
            pltpu.VMEM((2, ways, feat, BLOCK), BF),
            pltpu.VMEM((ways, feat, BLOCK), BF),
            pltpu.SemaphoreType.DMA((2 * ways,)),
            pltpu.SemaphoreType.DMA((ways,)),
            pltpu.SemaphoreType.DMA((ways,)),
        ]
    return pl.pallas_call(
        functools.partial(chunk_kernel, spec),
        out_shape=tuple(out_shape),
        in_specs=[smem, smem] + [any_spec] * (moved - 2) + [hbm] * (len(args) - moved),
        out_specs=tuple(out_specs),
        scratch_shapes=scratch,
        input_output_aliases=aliases,
        compiler_params=pltpu.CompilerParams(vmem_limit_bytes=44 << 20),
        cost_estimate=pl.CostEstimate(
            flops=flops, transcendentals=points * 1024, bytes_accessed=points * width * 4 + (4 << 20)
        ),
        name=f"layer_chunk_{first_window}",
    )(*args[:moved], *in_hbm(args[moved:]))


def in_hbm(arrays):
    return [pltpu.with_memory_space_constraint(a, pltpu.HBM) for a in arrays]


def copy_run(piece, out, lower, size, first, limit, shift):
    def one(v, carry):
        out[v + shift] = piece[v - lower]
        return carry

    lax.fori_loop(jnp.maximum(first, lower), jnp.minimum(limit, lower + size), one, 0)


def place_kernel(kept_ref, *refs):
    count = (len(refs) - 3) // 2
    pieces_hbm, out_hbm, bufs, out, sems = (
        refs[:count],
        refs[count],
        refs[count + 1 : 2 * count + 1],
        refs[2 * count + 1],
        refs[2 * count + 2],
    )
    loads = [pltpu.make_async_copy(pieces_hbm[n], bufs[n], sems.at[n]) for n in range(count)]
    for c in loads:
        c.start()
    for c in loads:
        c.wait()
    own, came = bufs[: (count + 1) // 2], bufs[(count + 1) // 2 :]
    slots = out.shape[0]
    total = slots // 2
    kept = kept_ref[0] * 2
    kept_before = jnp.max(came[0][came[0].shape[0] - 1].astype(F32)).astype(jnp.int32) * 2
    blank = jnp.zeros(out.shape[1:], BF)

    def clear(v, carry):
        out[v] = blank
        return carry

    lax.fori_loop(kept + total - kept_before, slots, clear, 0)
    lower = 1
    for n, piece in enumerate(own):
        size = piece.shape[0] - (n == 0)
        copy_run(piece, out, lower, size, 0, jnp.minimum(kept, total), 0)
        lower += size
    lower = 1
    for n, piece in enumerate(came):
        size = piece.shape[0] - (n == 0)
        copy_run(piece, out, lower, size, kept_before, total, kept - kept_before)
        lower += size

    @pl.when(kept > 0)
    def _():
        out[0] = own[-1][own[-1].shape[0] - 1]

    c = pltpu.make_async_copy(out, out_hbm, sems.at[count])
    c.start()
    c.wait()


def final_kernel(kept_ref, piece, mark, _, out, sem):
    total = out.shape[0] // 2
    count = piece.shape[0]
    lower = total - (count - 3)
    kept = kept_ref[0] * 2
    kept_before = jnp.max(mark[mark.shape[0] - 1].astype(F32)).astype(jnp.int32) * 2
    shift = kept - kept_before

    def put(v, source):
        return pltpu.make_async_copy(piece.at[source], out.at[v + shift], sem.at[v])

    def start(v, carry):
        put(v, v - lower).start()
        return carry

    def wait(v, carry):
        put(v, v - lower).wait()
        return carry

    low = jnp.maximum(kept_before, lower)
    lax.fori_loop(low, total, start, 0)

    @pl.when(kept_before == 0)
    def _():
        put(0, count - 1).start()

    lax.fori_loop(low, total, wait, 0)

    @pl.when(kept_before == 0)
    def _():
        put(0, count - 1).wait()


def body(points, w_query, w_key, w_value, w_out, w_up, w_down, w_pool, keep_count):
    feat = points.shape[1]
    ways = lax.axis_size("mp")
    seq_ways = lax.axis_size("seq")
    quarter = points.shape[0] // ways
    pool_width = w_pool.shape[1]
    mp_index = lax.axis_index("mp").astype(jnp.int32)[None]
    own = points.T
    tiles_quarter = quarter // BLOCK
    last_chunk = len(CHUNKS) - 1

    spans = []
    tile = 0
    for n, windows in enumerate(CHUNKS):
        count = windows + 1 if n == 0 else windows
        if n == last_chunk:
            count = tiles_quarter - tile
        spans.append((tile, count))
        tile += count

    def exchange(block, shift):
        return lax.ppermute(block, "mp", [(i, i ^ shift) for i in range(ways)])

    edges = [(None, 0, 1), (None, own.shape[1] // BLOCK - 1, 1)]
    blocks = send_blocks(mp_index, own, quarter, [(s, *spans[0]) for s in SHIFTS] + edges, "first_blocks")
    received = [[exchange(b, s) for b, s in zip(blocks, SHIFTS)]]
    after = lax.ppermute(blocks[-2], "seq", [((i + 1) % seq_ways, i) for i in range(seq_ways)])
    prior = lax.ppermute(blocks[-1], "seq", [(i, (i + 1) % seq_ways) for i in range(seq_ways)])
    for n in range(1, last_chunk):
        blocks = send_blocks(mp_index, own, quarter, [(s, *spans[n]) for s in SHIFTS], f"blocks_{n}")
        received.append([exchange(b, s) for b, s in zip(blocks, SHIFTS)])

    pairs = [(i, (i + 1) % (seq_ways * ways)) for i in range(seq_ways * ways)]
    weights = [w_query, w_key, w_value, w_out, w_up, w_down, w_pool]
    refined = halo_own = None
    window = 1
    own_pooled, came_pooled = [], []
    for n, windows in enumerate(CHUNKS):
        tile, count = spans[n]
        spec = (tile, count, window, windows, n == last_chunk, n > 0, quarter, feat, spans[last_chunk])
        refined, pooled, *rest = run_chunk(
            spec,
            mp_index,
            keep_count,
            own,
            received[n],
            received[n - 1] if n else None,
            halo_own,
            received[0],
            came_pooled[0] if n else None,
            [after, prior],
            weights,
            refined,
            quarter,
        )
        own_pooled.append(pooled)
        came_pooled.append(lax.ppermute(pooled, ("seq", "mp"), pairs))
        window += windows
        if n == 0:
            halo_own = rest[-1]
            received.append([exchange(b, s) for b, s in zip(rest, SHIFTS)])

    slots = 2 * quarter // (CHILDREN * 8)
    smem = pl.BlockSpec(memory_space=pltpu.SMEM)
    hbm = pl.BlockSpec(memory_space=pltpu.HBM)
    vmem = pl.BlockSpec(memory_space=pltpu.VMEM)
    shape = (slots, 8, pool_width)
    pieces = own_pooled + came_pooled[:-1]
    coarse = pl.pallas_call(
        place_kernel,
        out_shape=jax.ShapeDtypeStruct(shape, BF),
        in_specs=[smem] + [pl.BlockSpec(memory_space=pl.ANY)] * len(pieces),
        out_specs=hbm,
        scratch_shapes=[pltpu.VMEM(p.shape, BF) for p in pieces]
        + [pltpu.VMEM(shape, BF), pltpu.SemaphoreType.DMA((len(pieces) + 1,))],
        compiler_params=pltpu.CompilerParams(vmem_limit_bytes=16 << 20),
        name="place_tiles",
    )(keep_count, *pieces)
    coarse = pl.pallas_call(
        final_kernel,
        out_shape=jax.ShapeDtypeStruct(shape, BF),
        in_specs=[smem, vmem, vmem, hbm],
        out_specs=hbm,
        scratch_shapes=[pltpu.SemaphoreType.DMA((slots // 2,))],
        input_output_aliases={3: 0},
        name="place_final",
    )(
        keep_count,
        pltpu.with_memory_space_constraint(came_pooled[-1], pltpu.VMEM),
        pltpu.with_memory_space_constraint(came_pooled[0], pltpu.VMEM),
        *in_hbm([coarse]),
    )
    return (refined, coarse.reshape(slots * 8, pool_width))


def solution(mesh):
    placed = (
        P(("groups", "seq"), "mp"),
        P(),
        P(),
        P(),
        P(),
        P(),
        P(),
        P(),
        P(("groups", "seq", "mp")),
    )
    return jax.shard_map(
        body,
        mesh=mesh,
        in_specs=placed,
        out_specs=(P(("groups", "seq", "mp"), None), P(("groups", "seq", "mp"), None)),
        check_vma=False,
    )
```

```python
import functools
import math

import jax
import jax.numpy as jnp
from jax import lax
from jax.experimental import pallas as pl
from jax.experimental.pallas import tpu as pltpu
from jax.sharding import PartitionSpec as P

HEADS = 8
WINDOW = 32
DILATION = 4
TILE_PARENTS = 16
CHILDREN = 8
BLOCK = WINDOW * DILATION
HALF = BLOCK // 2
CHUNKS = (7, 13, 13)
FFN_ROWS = 384
FFN_COLS = 256
SHIFTS = (3, 2, 1)

BF = jnp.bfloat16
F32 = jnp.float32


def gather_order():
    row = lax.broadcasted_iota(jnp.int32, (BLOCK, 2 * BLOCK), 0)
    col = lax.broadcasted_iota(jnp.int32, (BLOCK, 2 * BLOCK), 1)
    return (col == HALF + DILATION * (row % WINDOW) + row // WINDOW).astype(F32).astype(BF)


def output_order():
    row = lax.broadcasted_iota(jnp.int32, (2 * BLOCK, BLOCK), 0)
    col = lax.broadcasted_iota(jnp.int32, (2 * BLOCK, BLOCK), 1)
    point = DILATION * (col % WINDOW) + col // WINDOW
    by_child = BLOCK + (point % CHILDREN) * TILE_PARENTS + point // CHILDREN
    return ((row == point) | (row == by_child)).astype(F32).astype(BF)


def head_mask(width):
    rows = HEADS * WINDOW
    row = lax.broadcasted_iota(jnp.int32, (rows, width), 0)
    col = lax.broadcasted_iota(jnp.int32, (rows, width), 1)
    return (row // (WINDOW // 2) % HEADS == col // (width // HEADS)).astype(F32).astype(BF)


def norm_rows(values):
    centre = values - jnp.mean(values, axis=-1, keepdims=True)
    spread = jnp.mean(centre * centre, axis=-1, keepdims=True)
    return centre * lax.rsqrt(spread + 1e-05)


def dot_nn(a, b):
    return lax.dot_general(a, b, (((1,), (0,)), ((), ())), preferred_element_type=F32)


def dot_nt(a, b):
    return lax.dot_general(a, b, (((1,), (1,)), ((), ())), preferred_element_type=F32)


def segment_max(scores):
    width = scores.shape[1] // 2
    run = WINDOW // 2
    top = jnp.maximum(scores[:, :width], scores[:, width:])
    for shift in (1, 2, 4, 8):
        top = jnp.maximum(top, pltpu.roll(top, shift, 1))
    lane = lax.broadcasted_iota(jnp.int32, top.shape, 1)
    top = jnp.where(lane % run == run - 1, top, -jnp.inf)
    for shift in (1, 2, 4, 8):
        top = jnp.maximum(top, pltpu.roll(top, width - shift, 1))
    return top


def feed_forward(hidden, normed, up_ref, down_ref):
    hidden_width = up_ref.shape[1]
    rows = hidden.shape[0]
    done = []
    for r in range(0, rows, FFN_ROWS):
        part = slice(r, min(r + FFN_ROWS, rows))
        total = hidden[part]
        for c in range(0, hidden_width, FFN_COLS):
            up = dot_nn(normed[part], up_ref[:, c : c + FFN_COLS])
            inner = up * (0.7978845608028654 + 0.035677408136300125 * (up * up))
            half = 0.5 * up
            activated = (half + half * jnp.tanh(inner)).astype(BF)
            total = total + dot_nn(activated, down_ref[c : c + FFN_COLS, :])
        done.append(total.astype(BF))
    return jnp.concatenate(done, axis=0)


def layer(x, weights, arrive, windows):
    wq, wk, wv, wo, wu, wd = weights
    width = x.shape[1]
    normed = norm_rows(x).astype(BF)
    arrive(0, 3)
    queries = dot_nn(normed, wq[...]).astype(BF)
    keys = dot_nn(normed, wk[...]).astype(BF)
    values = dot_nn(normed, wv[...]).astype(BF)
    mask = head_mask(width)
    run = WINDOW // 2
    groups = windows * DILATION
    scores = []
    for g in range(groups):
        rows = slice(g * WINDOW, (g + 1) * WINDOW)
        k = keys[rows]
        wide = jnp.concatenate([k[:run]] * HEADS + [k[run:]] * HEADS, axis=0) * mask
        scores.append(dot_nt(queries[rows], wide))
    scores = jnp.concatenate(scores, axis=0)
    top = segment_max(scores)
    top = jnp.concatenate([top, top], axis=1)
    factor = math.log2(math.e) / math.sqrt(width // HEADS)
    shares = jnp.exp2((scores - top) * factor).astype(BF)
    total = dot_nn(shares, mask)
    mixed = []
    for g in range(groups):
        rows = slice(g * WINDOW, (g + 1) * WINDOW)
        v = values[rows]
        wide = jnp.concatenate([v[:run]] * HEADS + [v[run:]] * HEADS, axis=0) * mask
        mixed.append(dot_nn(shares[rows], wide))
    attended = (jnp.concatenate(mixed, axis=0) / total).astype(BF)
    arrive(3, 6)
    hidden = x + dot_nn(attended, wo[...])
    return feed_forward(hidden, norm_rows(hidden).astype(BF), wu, wd)


def send_kernel(quarter, wanted, mp_ref, own, *refs):
    count = len(wanted)
    outs, bufs, sems = refs[:count], refs[count : 2 * count], refs[2 * count]
    loads, puts = [], []
    for n, (shift, tile, tiles, free) in enumerate(wanted):
        col = tile * BLOCK
        if shift is not None:
            col = pl.multiple_of((mp_ref[0] ^ shift) * quarter + col, BLOCK)
        loads.append(pltpu.make_async_copy(own.at[:, pl.ds(col, tiles * BLOCK)], bufs[n], sems.at[0, n]))
        dst = outs[n].at[:, pl.ds(0, tiles * BLOCK)] if free else outs[n]
        puts.append(pltpu.make_async_copy(bufs[n], dst, sems.at[1, n]))
    for c in loads:
        c.start()
    for load, put in zip(loads, puts):
        load.wait()
        put.start()
    for c in puts:
        c.wait()


def send_blocks(mp_index, own, quarter, wanted, name):
    hbm = pl.BlockSpec(memory_space=pltpu.HBM)
    return pl.pallas_call(
        functools.partial(send_kernel, quarter, wanted),
        out_shape=tuple(jax.ShapeDtypeStruct((own.shape[0], (t + f) * BLOCK), BF) for _, _, t, f in wanted),
        in_specs=[pl.BlockSpec(memory_space=pltpu.SMEM), hbm],
        out_specs=(hbm,) * len(wanted),
        scratch_shapes=[pltpu.VMEM((own.shape[0], t * BLOCK), BF) for _, _, t, _ in wanted]
        + [pltpu.SemaphoreType.DMA((2, len(wanted)))],
        name=name,
    )(mp_index, *in_hbm([own]))


def last_blocks(spec, mp_index, own, after, prior, outs, edge, halo, edge_sems, put_sems):
    quarter, ways, tiles = spec
    edges = []
    for q in range(ways):
        head = own.at[:, pl.ds((q + 1) * quarter, BLOCK)] if q + 1 < ways else after
        tail = own.at[:, pl.ds(q * quarter - BLOCK, BLOCK)] if q else prior
        edges.append(pltpu.make_async_copy(head, edge.at[0, q], edge_sems.at[2 * q]))
        edges.append(pltpu.make_async_copy(tail, edge.at[1, q], edge_sems.at[2 * q + 1]))
    puts = []
    for n in range(ways - 1):
        dst = outs[n].at[:, pl.ds(tiles * BLOCK, BLOCK)]
        puts.append(pltpu.make_async_copy(halo.at[mp_index ^ SHIFTS[n]], dst, put_sems.at[n]))
    puts.append(pltpu.make_async_copy(halo.at[mp_index], outs[ways - 1], put_sems.at[ways - 1]))

    def begin():
        for c in edges:
            c.start()

    def send():
        for c in edges:
            c.wait()
        lane = lax.broadcasted_iota(jnp.int32, edge.shape[1:], 2)
        halo[...] = jnp.where(lane < HALF, edge[0].astype(F32), edge[1].astype(F32)).astype(BF)
        for c in puts:
            c.start()

    def end():
        for c in puts:
            c.wait()

    return begin, send, end


def chunk_kernel(spec, *refs):
    first_tile, tiles, first_window, windows, last, aliased, marked, quarter, feat, last_span = spec
    n_recv = 3
    it = iter(refs)
    place_ref = next(it)
    kept_ref = next(it)
    own = next(it)
    recv = [next(it) for _ in range(n_recv)]
    if first_window > 1:
        before = [next(it) for _ in range(n_recv)]
    if last:
        halo_own = next(it)
        start = [next(it) for _ in range(n_recv)]
    elif aliased:
        pooled_before = next(it)
    if not aliased:
        after, prior = next(it), next(it)
        for _ in range(n_recv):
            next(it)
    weights_hbm = [next(it) for _ in range(7)]
    if aliased:
        next(it)
    refined, pooled = next(it), next(it)
    if not aliased:
        block_outs = [next(it) for _ in range(n_recv + 1)]
    xbuf, ybuf, pbuf, pooled_buf = (next(it) for _ in range(4))
    weights = [next(it) for _ in range(7)]
    in_sem, w_sem, out_sem, pool_sem = (next(it) for _ in range(4))
    mp_index = place_ref[0]
    if not aliased:
        begin, send, end = last_blocks(
            (quarter, n_recv + 1, last_span[1]), mp_index, own, after, prior, block_outs, *it
        )
    copies = []
    kept_halves = pooled_before.shape[0] if aliased and not last else 0
    fetch = [pltpu.make_async_copy(weights_hbm[n], weights[n], w_sem.at[n]) for n in range(7)]

    def arrive(first, limit):
        for n in range(first, limit):
            fetch[n].wait()
        if first == 3 and not aliased:
            send()

    def bring(src, shift, col, width):
        j = mp_index ^ shift
        dst = xbuf.at[pl.ds(pl.multiple_of(j * feat, feat), feat), pl.ds(col, width)]
        c = pltpu.make_async_copy(src, dst, in_sem.at[len(copies)])
        c.start()
        copies.append(c)

    def own_cols(tile, count):
        return own.at[:, pl.ds(pl.multiple_of(mp_index * quarter + tile * BLOCK, BLOCK), count * BLOCK)]

    lead = 0
    if first_window > 1:
        lead = 1
        for s in range(n_recv):
            n_before = before[s].shape[1]
            bring(before[s].at[:, pl.ds(n_before - BLOCK, BLOCK)], n_recv - s, 0, BLOCK)
        bring(own_cols(first_tile - 1, 1), 0, 0, BLOCK)
    for s in range(n_recv):
        bring(recv[s], n_recv - s, lead * BLOCK, recv[s].shape[1])
    bring(own_cols(first_tile, tiles), 0, lead * BLOCK, tiles * BLOCK)
    if last:
        bring(halo_own, 0, (lead + tiles) * BLOCK, BLOCK)
        for s in range(n_recv):
            bring(start[s].at[:, pl.ds(0, BLOCK)], n_recv - s, (lead + tiles + 1) * BLOCK, BLOCK)
        bring(own_cols(0, 1), 0, (lead + tiles + 1) * BLOCK, BLOCK)
    for n in range(3):
        fetch[n].start()
    gather = gather_order()
    back = output_order()
    for c in copies:
        c.wait()
    for n in range(3, 7):
        fetch[n].start()
    if not aliased:
        begin()
    if kept_halves:
        carried = pltpu.make_async_copy(pooled_before, pooled_buf.at[pl.ds(0, kept_halves)], pool_sem.at[1])
        carried.start()

    width = 4 * feat
    xs = [dot_nt(gather, xbuf[:, n * BLOCK : (n + 2) * BLOCK]) for n in range(windows)]
    ys = layer(jnp.concatenate(xs, axis=0), weights[:6], arrive, windows)
    for n in range(windows):
        both = dot_nn(back, ys[n * BLOCK : (n + 1) * BLOCK]).astype(BF)
        ybuf[n * BLOCK : (n + 1) * BLOCK, :] = both[:BLOCK]
        for c in range(CHILDREN):
            piece = both[BLOCK + c * TILE_PARENTS : BLOCK + (c + 1) * TILE_PARENTS]
            pbuf[n * TILE_PARENTS : (n + 1) * TILE_PARENTS, c * width : (c + 1) * width] = piece
    base = first_window * BLOCK - HALF
    outs = []
    if last:
        rows = quarter - base
        outs.append(pltpu.make_async_copy(ybuf.at[pl.ds(0, rows)], refined.at[pl.ds(base, rows)], out_sem.at[0]))
        outs.append(
            pltpu.make_async_copy(
                ybuf.at[pl.ds(windows * BLOCK - HALF, HALF)], refined.at[pl.ds(0, HALF)], out_sem.at[1]
            )
        )
    else:
        rows = windows * BLOCK
        outs.append(pltpu.make_async_copy(ybuf, refined.at[pl.ds(base, rows)], out_sem.at[0]))
    for c in outs:
        c.start()
    arrive(6, 7)
    result = dot_nn(pbuf[...], weights[6][...])
    halves = windows * TILE_PARENTS // 8
    result = result.reshape((halves,) + pooled_buf.shape[1:]).astype(BF)
    pooled_buf[kept_halves : kept_halves + halves] = result
    if marked:
        pooled_buf[kept_halves + halves] = jnp.full(pooled_buf.shape[1:], kept_ref[0], jnp.int32).astype(F32).astype(BF)
    if kept_halves:
        carried.wait()
    c = pltpu.make_async_copy(pooled_buf, pooled, pool_sem.at[0])
    c.start()
    c.wait()
    for c in outs:
        c.wait()
    if not aliased:
        end()


def run_chunk(spec, mp_index, kept, own, recv, before, halo_own, start, pooled_before, edges, weights, refined, rows):
    first_tile, tiles, first_window, windows, last, aliased, marked, quarter, feat, last_span = spec
    width = 4 * feat
    pool_width = weights[6].shape[1]
    smem = pl.BlockSpec(memory_space=pltpu.SMEM)
    hbm = pl.BlockSpec(memory_space=pltpu.HBM)
    any_spec = pl.BlockSpec(memory_space=pl.ANY)
    args = [mp_index, kept] + in_hbm([own]) + recv
    if first_window > 1:
        args += before
    if last:
        args += [halo_own] + start
    elif aliased:
        args.append(pooled_before)
    aliases = {}
    if not aliased:
        args += edges[:2]
        for n, block in enumerate(in_hbm(edges[2:])):
            aliases[len(args)] = 2 + n
            args.append(block)
    moved = len(args)
    args += weights
    if aliased:
        aliases = {len(args): 0}
        args.append(refined)
    halves = windows * TILE_PARENTS // 8
    points = windows * BLOCK
    flops = 2 * points * (width * width * 16 + 2 * width * weights[4].shape[1] + width * pool_width)
    before_halves = pooled_before.shape[0] if aliased and not last else 0
    piece = (before_halves + halves + int(marked), 8, pool_width)
    out_shape = [jax.ShapeDtypeStruct((rows, width), BF), jax.ShapeDtypeStruct(piece, BF)]
    out_specs = [hbm, any_spec]
    scratch = [
        pltpu.VMEM((width, (windows + 1) * BLOCK), BF),
        pltpu.VMEM((points, width), BF),
        pltpu.VMEM((windows * TILE_PARENTS, CHILDREN * width), BF),
        pltpu.VMEM(piece, BF),
    ]
    scratch += [pltpu.VMEM(w.shape, BF) for w in weights]
    scratch += [
        pltpu.SemaphoreType.DMA((16,)),
        pltpu.SemaphoreType.DMA((7,)),
        pltpu.SemaphoreType.DMA((2,)),
        pltpu.SemaphoreType.DMA((2,)),
    ]
    if not aliased:
        ways = len(recv) + 1
        wide = (feat, (last_span[1] + 1) * BLOCK)
        out_shape += [jax.ShapeDtypeStruct(wide, BF)] * len(recv) + [jax.ShapeDtypeStruct((feat, BLOCK), BF)]
        out_specs += [hbm] * len(recv) + [any_spec]
        scratch += [
            pltpu.VMEM((2, ways, feat, BLOCK), BF),
            pltpu.VMEM((ways, feat, BLOCK), BF),
            pltpu.SemaphoreType.DMA((2 * ways,)),
            pltpu.SemaphoreType.DMA((ways,)),
        ]
    return pl.pallas_call(
        functools.partial(chunk_kernel, spec),
        out_shape=tuple(out_shape),
        in_specs=[smem, smem] + [any_spec] * (moved - 2) + [hbm] * (len(args) - moved),
        out_specs=tuple(out_specs),
        scratch_shapes=scratch,
        input_output_aliases=aliases,
        compiler_params=pltpu.CompilerParams(vmem_limit_bytes=44 << 20),
        cost_estimate=pl.CostEstimate(
            flops=flops, transcendentals=points * 1024, bytes_accessed=points * width * 4 + (4 << 20)
        ),
        name=f"layer_chunk_{first_window}",
    )(*args[:moved], *in_hbm(args[moved:]))


def in_hbm(arrays):
    return [pltpu.with_memory_space_constraint(a, pltpu.HBM) for a in arrays]


def copy_run(piece, out, lower, size, first, limit, shift):
    def one(v, carry):
        out[v + shift] = piece[v - lower]
        return carry

    lax.fori_loop(jnp.maximum(first, lower), jnp.minimum(limit, lower + size), one, 0)


def place_kernel(kept_ref, *refs):
    count = (len(refs) - 3) // 2
    pieces_hbm, out_hbm, bufs, out, sems = (
        refs[:count],
        refs[count],
        refs[count + 1 : 2 * count + 1],
        refs[2 * count + 1],
        refs[2 * count + 2],
    )
    loads = [pltpu.make_async_copy(pieces_hbm[n], bufs[n], sems.at[n]) for n in range(count)]
    for c in loads:
        c.start()
    for c in loads:
        c.wait()
    own, came = bufs[: (count + 1) // 2], bufs[(count + 1) // 2 :]
    slots = out.shape[0]
    total = slots // 2
    kept = kept_ref[0] * 2
    kept_before = jnp.max(came[0][came[0].shape[0] - 1].astype(F32)).astype(jnp.int32) * 2
    blank = jnp.zeros(out.shape[1:], BF)

    def clear(v, carry):
        out[v] = blank
        return carry

    lax.fori_loop(kept + total - kept_before, slots, clear, 0)
    lower = 1
    for n, piece in enumerate(own):
        size = piece.shape[0] - (n == 0)
        copy_run(piece, out, lower, size, 0, jnp.minimum(kept, total), 0)
        lower += size
    lower = 1
    for n, piece in enumerate(came):
        size = piece.shape[0] - (n == 0)
        copy_run(piece, out, lower, size, kept_before, total, kept - kept_before)
        lower += size

    @pl.when(kept > 0)
    def _():
        out[0] = own[-1][own[-1].shape[0] - 1]

    c = pltpu.make_async_copy(out, out_hbm, sems.at[count])
    c.start()
    c.wait()


def final_kernel(kept_ref, piece, mark, _, out, sem):
    total = out.shape[0] // 2
    count = piece.shape[0]
    lower = total - (count - 3)
    kept = kept_ref[0] * 2
    kept_before = jnp.max(mark[mark.shape[0] - 1].astype(F32)).astype(jnp.int32) * 2
    shift = kept - kept_before

    def put(v, source):
        return pltpu.make_async_copy(piece.at[source], out.at[v + shift], sem.at[v])

    def start(v, carry):
        put(v, v - lower).start()
        return carry

    def wait(v, carry):
        put(v, v - lower).wait()
        return carry

    low = jnp.maximum(kept_before, lower)
    lax.fori_loop(low, total, start, 0)

    @pl.when(kept_before == 0)
    def _():
        put(0, count - 1).start()

    lax.fori_loop(low, total, wait, 0)

    @pl.when(kept_before == 0)
    def _():
        put(0, count - 1).wait()


def body(points, w_query, w_key, w_value, w_out, w_up, w_down, w_pool, keep_count):
    feat = points.shape[1]
    ways = lax.axis_size("mp")
    seq_ways = lax.axis_size("seq")
    quarter = points.shape[0] // ways
    pool_width = w_pool.shape[1]
    mp_index = lax.axis_index("mp").astype(jnp.int32)[None]
    own = points.T
    tiles_quarter = quarter // BLOCK
    last_chunk = len(CHUNKS) - 1

    spans = []
    tile = 0
    for n, windows in enumerate(CHUNKS):
        count = windows + 1 if n == 0 else windows
        if n == last_chunk:
            count = tiles_quarter - tile
        spans.append((tile, count))
        tile += count

    def exchange(block, shift):
        return lax.ppermute(block, "mp", [(i, i ^ shift) for i in range(ways)])

    edges = [(None, 0, 1, 0), (None, own.shape[1] // BLOCK - 1, 1, 0)]
    blocks = send_blocks(mp_index, own, quarter, [(s, *spans[0], 0) for s in SHIFTS] + edges, "first_blocks")
    received = [[exchange(b, s) for b, s in zip(blocks, SHIFTS)]]
    after = lax.ppermute(blocks[-2], "seq", [((i + 1) % seq_ways, i) for i in range(seq_ways)])
    prior = lax.ppermute(blocks[-1], "seq", [(i, (i + 1) % seq_ways) for i in range(seq_ways)])
    wanted = [(s, *spans[n], int(n == last_chunk)) for n in range(1, last_chunk + 1) for s in SHIFTS]
    blocks = list(send_blocks(mp_index, own, quarter, wanted, "later_blocks"))
    for n in range(last_chunk - 1):
        received.append([exchange(blocks[n * len(SHIFTS) + m], s) for m, s in enumerate(SHIFTS)])
    unfinished = blocks[-len(SHIFTS) :]

    pairs = [(i, (i + 1) % (seq_ways * ways)) for i in range(seq_ways * ways)]
    weights = [w_query, w_key, w_value, w_out, w_up, w_down, w_pool]
    refined = halo_own = pooled = None
    window = 1
    own_pooled, came_pooled = [], []
    for n, windows in enumerate(CHUNKS):
        tile, count = spans[n]
        spec = (tile, count, window, windows, n == last_chunk, n > 0, n == last_chunk - 1, quarter, feat, spans[last_chunk])
        refined, pooled, *rest = run_chunk(
            spec,
            mp_index,
            keep_count,
            own,
            received[n],
            received[n - 1] if n else None,
            halo_own,
            received[0],
            pooled,
            [after, prior] + unfinished,
            weights,
            refined,
            quarter,
        )
        if n >= last_chunk - 1:
            own_pooled.append(pooled)
            came_pooled.append(lax.ppermute(pooled, ("seq", "mp"), pairs))
        window += windows
        if n == 0:
            halo_own = rest[-1]
            received.append([exchange(b, s) for b, s in zip(rest, SHIFTS)])

    slots = 2 * quarter // (CHILDREN * 8)
    smem = pl.BlockSpec(memory_space=pltpu.SMEM)
    hbm = pl.BlockSpec(memory_space=pltpu.HBM)
    vmem = pl.BlockSpec(memory_space=pltpu.VMEM)
    shape = (slots, 8, pool_width)
    pieces = own_pooled + came_pooled[:-1]
    coarse = pl.pallas_call(
        place_kernel,
        out_shape=jax.ShapeDtypeStruct(shape, BF),
        in_specs=[smem] + [pl.BlockSpec(memory_space=pl.ANY)] * len(pieces),
        out_specs=hbm,
        scratch_shapes=[pltpu.VMEM(p.shape, BF) for p in pieces]
        + [pltpu.VMEM(shape, BF), pltpu.SemaphoreType.DMA((len(pieces) + 1,))],
        compiler_params=pltpu.CompilerParams(vmem_limit_bytes=16 << 20),
        name="place_tiles",
    )(keep_count, *pieces)
    coarse = pl.pallas_call(
        final_kernel,
        out_shape=jax.ShapeDtypeStruct(shape, BF),
        in_specs=[smem, vmem, vmem, hbm],
        out_specs=hbm,
        scratch_shapes=[pltpu.SemaphoreType.DMA((slots // 2,))],
        input_output_aliases={3: 0},
        name="place_final",
    )(
        keep_count,
        pltpu.with_memory_space_constraint(came_pooled[-1], pltpu.VMEM),
        pltpu.with_memory_space_constraint(came_pooled[0], pltpu.VMEM),
        *in_hbm([coarse]),
    )
    return (refined, coarse.reshape(slots * 8, pool_width))


def solution(mesh):
    placed = (
        P(("groups", "seq"), "mp"),
        P(),
        P(),
        P(),
        P(),
        P(),
        P(),
        P(),
        P(("groups", "seq", "mp")),
    )
    return jax.shard_map(
        body,
        mesh=mesh,
        in_specs=placed,
        out_specs=(P(("groups", "seq", "mp"), None), P(("groups", "seq", "mp"), None)),
        check_vma=False,
    )
```

```python
import functools
import math

import jax
import jax.numpy as jnp
from jax import lax
from jax.experimental import pallas as pl
from jax.experimental.pallas import tpu as pltpu
from jax.sharding import PartitionSpec as P

HEADS = 8
WINDOW = 32
DILATION = 4
TILE_PARENTS = 16
CHILDREN = 8
BLOCK = WINDOW * DILATION
HALF = BLOCK // 2
CHUNKS = (7, 13, 13)
FFN_ROWS = 384
FFN_COLS = 256
SHIFTS = (3, 2, 1)

BF = jnp.bfloat16
F32 = jnp.float32


def gather_order():
    row = lax.broadcasted_iota(jnp.int32, (BLOCK, 2 * BLOCK), 0)
    col = lax.broadcasted_iota(jnp.int32, (BLOCK, 2 * BLOCK), 1)
    return (col == HALF + DILATION * (row % WINDOW) + row // WINDOW).astype(F32).astype(BF)


def output_order():
    row = lax.broadcasted_iota(jnp.int32, (2 * BLOCK, BLOCK), 0)
    col = lax.broadcasted_iota(jnp.int32, (2 * BLOCK, BLOCK), 1)
    point = DILATION * (col % WINDOW) + col // WINDOW
    by_child = BLOCK + (point % CHILDREN) * TILE_PARENTS + point // CHILDREN
    return ((row == point) | (row == by_child)).astype(F32).astype(BF)


def head_mask(width):
    rows = HEADS * WINDOW
    row = lax.broadcasted_iota(jnp.int32, (rows, width), 0)
    col = lax.broadcasted_iota(jnp.int32, (rows, width), 1)
    return (row // (WINDOW // 2) % HEADS == col // (width // HEADS)).astype(F32).astype(BF)


def norm_rows(values):
    centre = values - jnp.mean(values, axis=-1, keepdims=True)
    spread = jnp.mean(centre * centre, axis=-1, keepdims=True)
    return centre * lax.rsqrt(spread + 1e-05)


def dot_nn(a, b):
    return lax.dot_general(a, b, (((1,), (0,)), ((), ())), preferred_element_type=F32)


def dot_nt(a, b):
    return lax.dot_general(a, b, (((1,), (1,)), ((), ())), preferred_element_type=F32)


def segment_max(scores):
    width = scores.shape[1] // 2
    run = WINDOW // 2
    top = jnp.maximum(scores[:, :width], scores[:, width:])
    for shift in (1, 2, 4, 8):
        top = jnp.maximum(top, pltpu.roll(top, shift, 1))
    lane = lax.broadcasted_iota(jnp.int32, top.shape, 1)
    top = jnp.where(lane % run == run - 1, top, -jnp.inf)
    for shift in (1, 2, 4, 8):
        top = jnp.maximum(top, pltpu.roll(top, width - shift, 1))
    return top


def feed_forward(hidden, normed, up_ref, down_ref):
    hidden_width = up_ref.shape[1]
    rows = hidden.shape[0]
    done = []
    for r in range(0, rows, FFN_ROWS):
        part = slice(r, min(r + FFN_ROWS, rows))
        total = hidden[part]
        for c in range(0, hidden_width, FFN_COLS):
            up = dot_nn(normed[part], up_ref[:, c : c + FFN_COLS])
            inner = up * (0.7978845608028654 + 0.035677408136300125 * (up * up))
            half = 0.5 * up
            activated = (half + half * jnp.tanh(inner)).astype(BF)
            total = total + dot_nn(activated, down_ref[c : c + FFN_COLS, :])
        done.append(total.astype(BF))
    return jnp.concatenate(done, axis=0)


def layer(x, weights, arrive, windows):
    wq, wk, wv, wo, wu, wd = weights
    width = x.shape[1]
    normed = norm_rows(x).astype(BF)
    arrive(0, 3)
    queries = dot_nn(normed, wq[...]).astype(BF)
    keys = dot_nn(normed, wk[...]).astype(BF)
    values = dot_nn(normed, wv[...]).astype(BF)
    mask = head_mask(width)
    run = WINDOW // 2
    groups = windows * DILATION
    scores = []
    for g in range(groups):
        rows = slice(g * WINDOW, (g + 1) * WINDOW)
        k = keys[rows]
        wide = jnp.concatenate([k[:run]] * HEADS + [k[run:]] * HEADS, axis=0) * mask
        scores.append(dot_nt(queries[rows], wide))
    scores = jnp.concatenate(scores, axis=0)
    top = segment_max(scores)
    top = jnp.concatenate([top, top], axis=1)
    factor = math.log2(math.e) / math.sqrt(width // HEADS)
    shares = jnp.exp2((scores - top) * factor).astype(BF)
    total = dot_nn(shares, mask)
    mixed = []
    for g in range(groups):
        rows = slice(g * WINDOW, (g + 1) * WINDOW)
        v = values[rows]
        wide = jnp.concatenate([v[:run]] * HEADS + [v[run:]] * HEADS, axis=0) * mask
        mixed.append(dot_nn(shares[rows], wide))
    attended = (jnp.concatenate(mixed, axis=0) * pl.reciprocal(total)).astype(BF)
    arrive(3, 6)
    hidden = x + dot_nn(attended, wo[...])
    return feed_forward(hidden, norm_rows(hidden).astype(BF), wu, wd)


def send_kernel(quarter, wanted, mp_ref, own, *refs):
    count = len(wanted)
    outs, bufs, sems = refs[:count], refs[count : 2 * count], refs[2 * count]
    loads, puts = [], []
    for n, (shift, tile, tiles, free) in enumerate(wanted):
        col = tile * BLOCK
        if shift is not None:
            col = pl.multiple_of((mp_ref[0] ^ shift) * quarter + col, BLOCK)
        loads.append(pltpu.make_async_copy(own.at[:, pl.ds(col, tiles * BLOCK)], bufs[n], sems.at[0, n]))
        dst = outs[n].at[:, pl.ds(0, tiles * BLOCK)] if free else outs[n]
        puts.append(pltpu.make_async_copy(bufs[n], dst, sems.at[1, n]))
    for c in loads:
        c.start()
    for load, put in zip(loads, puts):
        load.wait()
        put.start()
    for c in puts:
        c.wait()


def send_blocks(mp_index, own, quarter, wanted, name):
    hbm = pl.BlockSpec(memory_space=pltpu.HBM)
    return pl.pallas_call(
        functools.partial(send_kernel, quarter, wanted),
        out_shape=tuple(jax.ShapeDtypeStruct((own.shape[0], (t + f) * BLOCK), BF) for _, _, t, f in wanted),
        in_specs=[pl.BlockSpec(memory_space=pltpu.SMEM), hbm],
        out_specs=(hbm,) * len(wanted),
        scratch_shapes=[pltpu.VMEM((own.shape[0], t * BLOCK), BF) for _, _, t, _ in wanted]
        + [pltpu.SemaphoreType.DMA((2, len(wanted)))],
        name=name,
    )(mp_index, *in_hbm([own]))


def last_blocks(spec, mp_index, own, after, prior, outs, edge, halo, edge_sems, put_sems):
    quarter, ways, tiles = spec
    edges = []
    for q in range(ways):
        head = own.at[:, pl.ds((q + 1) * quarter, BLOCK)] if q + 1 < ways else after
        tail = own.at[:, pl.ds(q * quarter - BLOCK, BLOCK)] if q else prior
        edges.append(pltpu.make_async_copy(head, edge.at[0, q], edge_sems.at[2 * q]))
        edges.append(pltpu.make_async_copy(tail, edge.at[1, q], edge_sems.at[2 * q + 1]))
    puts = []
    for n in range(ways - 1):
        dst = outs[n].at[:, pl.ds(tiles * BLOCK, BLOCK)]
        puts.append(pltpu.make_async_copy(halo.at[mp_index ^ SHIFTS[n]], dst, put_sems.at[n]))
    puts.append(pltpu.make_async_copy(halo.at[mp_index], outs[ways - 1], put_sems.at[ways - 1]))

    def begin():
        for c in edges:
            c.start()

    def send():
        for c in edges:
            c.wait()
        lane = lax.broadcasted_iota(jnp.int32, edge.shape[1:], 2)
        halo[...] = jnp.where(lane < HALF, edge[0].astype(F32), edge[1].astype(F32)).astype(BF)
        for c in puts:
            c.start()

    def end():
        for c in puts:
            c.wait()

    return begin, send, end


def chunk_kernel(spec, *refs):
    first_tile, tiles, first_window, windows, last, aliased, marked, quarter, feat, last_span = spec
    n_recv = 3
    it = iter(refs)
    place_ref = next(it)
    kept_ref = next(it)
    own = next(it)
    recv = [next(it) for _ in range(n_recv)]
    if first_window > 1:
        before = [next(it) for _ in range(n_recv)]
    if last:
        halo_own = next(it)
        start = [next(it) for _ in range(n_recv)]
    elif aliased:
        pooled_before = next(it)
    if not aliased:
        after, prior = next(it), next(it)
        for _ in range(n_recv):
            next(it)
    weights_hbm = [next(it) for _ in range(7)]
    if aliased:
        next(it)
    refined, pooled = next(it), next(it)
    if not aliased:
        block_outs = [next(it) for _ in range(n_recv + 1)]
    xbuf, ybuf, pbuf, pooled_buf = (next(it) for _ in range(4))
    weights = [next(it) for _ in range(7)]
    in_sem, w_sem, out_sem, pool_sem = (next(it) for _ in range(4))
    mp_index = place_ref[0]
    if not aliased:
        begin, send, end = last_blocks(
            (quarter, n_recv + 1, last_span[1]), mp_index, own, after, prior, block_outs, *it
        )
    copies = []
    kept_halves = pooled_before.shape[0] if aliased and not last else 0
    fetch = [pltpu.make_async_copy(weights_hbm[n], weights[n], w_sem.at[n]) for n in range(7)]

    def arrive(first, limit):
        for n in range(first, limit):
            fetch[n].wait()
        if first == 3 and not aliased:
            send()

    def bring(src, shift, col, width):
        j = mp_index ^ shift
        dst = xbuf.at[pl.ds(pl.multiple_of(j * feat, feat), feat), pl.ds(col, width)]
        c = pltpu.make_async_copy(src, dst, in_sem.at[len(copies)])
        c.start()
        copies.append(c)

    def own_cols(tile, count):
        return own.at[:, pl.ds(pl.multiple_of(mp_index * quarter + tile * BLOCK, BLOCK), count * BLOCK)]

    lead = 0
    if first_window > 1:
        lead = 1
        for s in range(n_recv):
            n_before = before[s].shape[1]
            bring(before[s].at[:, pl.ds(n_before - BLOCK, BLOCK)], n_recv - s, 0, BLOCK)
        bring(own_cols(first_tile - 1, 1), 0, 0, BLOCK)
    for s in range(n_recv):
        bring(recv[s], n_recv - s, lead * BLOCK, recv[s].shape[1])
    bring(own_cols(first_tile, tiles), 0, lead * BLOCK, tiles * BLOCK)
    if last:
        bring(halo_own, 0, (lead + tiles) * BLOCK, BLOCK)
        for s in range(n_recv):
            bring(start[s].at[:, pl.ds(0, BLOCK)], n_recv - s, (lead + tiles + 1) * BLOCK, BLOCK)
        bring(own_cols(0, 1), 0, (lead + tiles + 1) * BLOCK, BLOCK)
    for n in range(3):
        fetch[n].start()
    gather = gather_order()
    back = output_order()
    for c in copies:
        c.wait()
    for n in range(3, 7):
        fetch[n].start()
    if not aliased:
        begin()
    if kept_halves:
        carried = pltpu.make_async_copy(pooled_before, pooled_buf.at[pl.ds(0, kept_halves)], pool_sem.at[1])
        carried.start()

    width = 4 * feat
    xs = [dot_nt(gather, xbuf[:, n * BLOCK : (n + 2) * BLOCK]) for n in range(windows)]
    ys = layer(jnp.concatenate(xs, axis=0), weights[:6], arrive, windows)
    for n in range(windows):
        both = dot_nn(back, ys[n * BLOCK : (n + 1) * BLOCK]).astype(BF)
        ybuf[n * BLOCK : (n + 1) * BLOCK, :] = both[:BLOCK]
        for c in range(CHILDREN):
            piece = both[BLOCK + c * TILE_PARENTS : BLOCK + (c + 1) * TILE_PARENTS]
            pbuf[n * TILE_PARENTS : (n + 1) * TILE_PARENTS, c * width : (c + 1) * width] = piece
    base = first_window * BLOCK - HALF
    outs = []
    if last:
        rows = quarter - base
        outs.append(pltpu.make_async_copy(ybuf.at[pl.ds(0, rows)], refined.at[pl.ds(base, rows)], out_sem.at[0]))
        outs.append(
            pltpu.make_async_copy(
                ybuf.at[pl.ds(windows * BLOCK - HALF, HALF)], refined.at[pl.ds(0, HALF)], out_sem.at[1]
            )
        )
    else:
        rows = windows * BLOCK
        outs.append(pltpu.make_async_copy(ybuf, refined.at[pl.ds(base, rows)], out_sem.at[0]))
    for c in outs:
        c.start()
    arrive(6, 7)
    result = dot_nn(pbuf[...], weights[6][...])
    halves = windows * TILE_PARENTS // 8
    result = result.reshape((halves,) + pooled_buf.shape[1:]).astype(BF)
    pooled_buf[kept_halves : kept_halves + halves] = result
    if marked:
        pooled_buf[kept_halves + halves] = jnp.full(pooled_buf.shape[1:], kept_ref[0], jnp.int32).astype(F32).astype(BF)
    if kept_halves:
        carried.wait()
    c = pltpu.make_async_copy(pooled_buf, pooled, pool_sem.at[0])
    c.start()
    c.wait()
    for c in outs:
        c.wait()
    if not aliased:
        end()


def run_chunk(spec, mp_index, kept, own, recv, before, halo_own, start, pooled_before, edges, weights, refined, rows):
    first_tile, tiles, first_window, windows, last, aliased, marked, quarter, feat, last_span = spec
    width = 4 * feat
    pool_width = weights[6].shape[1]
    smem = pl.BlockSpec(memory_space=pltpu.SMEM)
    hbm = pl.BlockSpec(memory_space=pltpu.HBM)
    any_spec = pl.BlockSpec(memory_space=pl.ANY)
    args = [mp_index, kept] + in_hbm([own]) + recv
    if first_window > 1:
        args += before
    if last:
        args += [halo_own] + start
    elif aliased:
        args.append(pooled_before)
    aliases = {}
    if not aliased:
        args += edges[:2]
        for n, block in enumerate(in_hbm(edges[2:])):
            aliases[len(args)] = 2 + n
            args.append(block)
    moved = len(args)
    args += weights
    if aliased:
        aliases = {len(args): 0}
        args.append(refined)
    halves = windows * TILE_PARENTS // 8
    points = windows * BLOCK
    flops = 2 * points * (width * width * 16 + 2 * width * weights[4].shape[1] + width * pool_width)
    before_halves = pooled_before.shape[0] if aliased and not last else 0
    piece = (before_halves + halves + int(marked), 8, pool_width)
    out_shape = [jax.ShapeDtypeStruct((rows, width), BF), jax.ShapeDtypeStruct(piece, BF)]
    out_specs = [hbm, any_spec]
    scratch = [
        pltpu.VMEM((width, (windows + 1) * BLOCK), BF),
        pltpu.VMEM((points, width), BF),
        pltpu.VMEM((windows * TILE_PARENTS, CHILDREN * width), BF),
        pltpu.VMEM(piece, BF),
    ]
    scratch += [pltpu.VMEM(w.shape, BF) for w in weights]
    scratch += [
        pltpu.SemaphoreType.DMA((16,)),
        pltpu.SemaphoreType.DMA((7,)),
        pltpu.SemaphoreType.DMA((2,)),
        pltpu.SemaphoreType.DMA((2,)),
    ]
    if not aliased:
        ways = len(recv) + 1
        wide = (feat, (last_span[1] + 1) * BLOCK)
        out_shape += [jax.ShapeDtypeStruct(wide, BF)] * len(recv) + [jax.ShapeDtypeStruct((feat, BLOCK), BF)]
        out_specs += [hbm] * len(recv) + [any_spec]
        scratch += [
            pltpu.VMEM((2, ways, feat, BLOCK), BF),
            pltpu.VMEM((ways, feat, BLOCK), BF),
            pltpu.SemaphoreType.DMA((2 * ways,)),
            pltpu.SemaphoreType.DMA((ways,)),
        ]
    return pl.pallas_call(
        functools.partial(chunk_kernel, spec),
        out_shape=tuple(out_shape),
        in_specs=[smem, smem] + [any_spec] * (moved - 2) + [hbm] * (len(args) - moved),
        out_specs=tuple(out_specs),
        scratch_shapes=scratch,
        input_output_aliases=aliases,
        compiler_params=pltpu.CompilerParams(vmem_limit_bytes=44 << 20),
        cost_estimate=pl.CostEstimate(
            flops=flops, transcendentals=points * 1024, bytes_accessed=points * width * 4 + (4 << 20)
        ),
        name=f"layer_chunk_{first_window}",
    )(*args[:moved], *in_hbm(args[moved:]))


def in_hbm(arrays):
    return [pltpu.with_memory_space_constraint(a, pltpu.HBM) for a in arrays]


def copy_run(piece, out, lower, size, first, limit, shift):
    def one(v, carry):
        out[v + shift] = piece[v - lower]
        return carry

    lax.fori_loop(jnp.maximum(first, lower), jnp.minimum(limit, lower + size), one, 0)


def place_kernel(kept_ref, *refs):
    count = (len(refs) - 3) // 2
    pieces_hbm, out_hbm, bufs, out, sems = (
        refs[:count],
        refs[count],
        refs[count + 1 : 2 * count + 1],
        refs[2 * count + 1],
        refs[2 * count + 2],
    )
    loads = [pltpu.make_async_copy(pieces_hbm[n], bufs[n], sems.at[n]) for n in range(count)]
    for c in loads:
        c.start()
    for c in loads:
        c.wait()
    own, came = bufs[: (count + 1) // 2], bufs[(count + 1) // 2 :]
    slots = out.shape[0]
    total = slots // 2
    kept = kept_ref[0] * 2
    kept_before = jnp.max(came[0][came[0].shape[0] - 1].astype(F32)).astype(jnp.int32) * 2
    blank = jnp.zeros(out.shape[1:], BF)

    def clear(v, carry):
        out[v] = blank
        return carry

    lax.fori_loop(kept + total - kept_before, slots, clear, 0)
    lower = 1
    for n, piece in enumerate(own):
        size = piece.shape[0] - (n == 0)
        copy_run(piece, out, lower, size, 0, jnp.minimum(kept, total), 0)
        lower += size
    lower = 1
    for n, piece in enumerate(came):
        size = piece.shape[0] - (n == 0)
        copy_run(piece, out, lower, size, kept_before, total, kept - kept_before)
        lower += size

    @pl.when(kept > 0)
    def _():
        out[0] = own[-1][own[-1].shape[0] - 1]

    c = pltpu.make_async_copy(out, out_hbm, sems.at[count])
    c.start()
    c.wait()


def final_kernel(kept_ref, piece, mark, _, out, sem):
    total = out.shape[0] // 2
    count = piece.shape[0]
    lower = total - (count - 3)
    kept = kept_ref[0] * 2
    kept_before = jnp.max(mark[mark.shape[0] - 1].astype(F32)).astype(jnp.int32) * 2
    shift = kept - kept_before

    def put(v, source):
        return pltpu.make_async_copy(piece.at[source], out.at[v + shift], sem.at[v])

    def start(v, carry):
        put(v, v - lower).start()
        return carry

    def wait(v, carry):
        put(v, v - lower).wait()
        return carry

    low = jnp.maximum(kept_before, lower)
    lax.fori_loop(low, total, start, 0)

    @pl.when(kept_before == 0)
    def _():
        put(0, count - 1).start()

    lax.fori_loop(low, total, wait, 0)

    @pl.when(kept_before == 0)
    def _():
        put(0, count - 1).wait()


def body(points, w_query, w_key, w_value, w_out, w_up, w_down, w_pool, keep_count):
    feat = points.shape[1]
    ways = lax.axis_size("mp")
    seq_ways = lax.axis_size("seq")
    quarter = points.shape[0] // ways
    pool_width = w_pool.shape[1]
    mp_index = lax.axis_index("mp").astype(jnp.int32)[None]
    own = points.T
    tiles_quarter = quarter // BLOCK
    last_chunk = len(CHUNKS) - 1

    spans = []
    tile = 0
    for n, windows in enumerate(CHUNKS):
        count = windows + 1 if n == 0 else windows
        if n == last_chunk:
            count = tiles_quarter - tile
        spans.append((tile, count))
        tile += count

    def exchange(block, shift):
        return lax.ppermute(block, "mp", [(i, i ^ shift) for i in range(ways)])

    edges = [(None, 0, 1, 0), (None, own.shape[1] // BLOCK - 1, 1, 0)]
    blocks = send_blocks(mp_index, own, quarter, [(s, *spans[0], 0) for s in SHIFTS], "first_blocks")
    received = [[exchange(b, s) for b, s in zip(blocks, SHIFTS)]]
    after = lax.ppermute(own[:, :BLOCK], "seq", [((i + 1) % seq_ways, i) for i in range(seq_ways)])
    prior = lax.ppermute(own[:, own.shape[1] - BLOCK :], "seq", [(i, (i + 1) % seq_ways) for i in range(seq_ways)])
    wanted = [(s, *spans[n], int(n == last_chunk)) for n in range(1, last_chunk + 1) for s in SHIFTS]
    blocks = list(send_blocks(mp_index, own, quarter, wanted, "later_blocks"))
    for n in range(last_chunk - 1):
        received.append([exchange(blocks[n * len(SHIFTS) + m], s) for m, s in enumerate(SHIFTS)])
    unfinished = blocks[-len(SHIFTS) :]

    pairs = [(i, (i + 1) % (seq_ways * ways)) for i in range(seq_ways * ways)]
    weights = [w_query, w_key, w_value, w_out, w_up, w_down, w_pool]
    refined = halo_own = pooled = None
    window = 1
    own_pooled, came_pooled = [], []
    for n, windows in enumerate(CHUNKS):
        tile, count = spans[n]
        spec = (tile, count, window, windows, n == last_chunk, n > 0, n == last_chunk - 1, quarter, feat, spans[last_chunk])
        refined, pooled, *rest = run_chunk(
            spec,
            mp_index,
            keep_count,
            own,
            received[n],
            received[n - 1] if n else None,
            halo_own,
            received[0],
            pooled,
            [after, prior] + unfinished,
            weights,
            refined,
            quarter,
        )
        if n >= last_chunk - 1:
            own_pooled.append(pooled)
            came_pooled.append(lax.ppermute(pooled, ("seq", "mp"), pairs))
        window += windows
        if n == 0:
            halo_own = rest[-1]
            received.append([exchange(b, s) for b, s in zip(rest, SHIFTS)])

    slots = 2 * quarter // (CHILDREN * 8)
    smem = pl.BlockSpec(memory_space=pltpu.SMEM)
    hbm = pl.BlockSpec(memory_space=pltpu.HBM)
    vmem = pl.BlockSpec(memory_space=pltpu.VMEM)
    shape = (slots, 8, pool_width)
    pieces = own_pooled + came_pooled[:-1]
    coarse = pl.pallas_call(
        place_kernel,
        out_shape=jax.ShapeDtypeStruct(shape, BF),
        in_specs=[smem] + [pl.BlockSpec(memory_space=pl.ANY)] * len(pieces),
        out_specs=hbm,
        scratch_shapes=[pltpu.VMEM(p.shape, BF) for p in pieces]
        + [pltpu.VMEM(shape, BF), pltpu.SemaphoreType.DMA((len(pieces) + 1,))],
        compiler_params=pltpu.CompilerParams(vmem_limit_bytes=16 << 20),
        name="place_tiles",
    )(keep_count, *pieces)
    coarse = pl.pallas_call(
        final_kernel,
        out_shape=jax.ShapeDtypeStruct(shape, BF),
        in_specs=[smem, vmem, vmem, hbm],
        out_specs=hbm,
        scratch_shapes=[pltpu.SemaphoreType.DMA((slots // 2,))],
        input_output_aliases={3: 0},
        name="place_final",
    )(
        keep_count,
        pltpu.with_memory_space_constraint(came_pooled[-1], pltpu.VMEM),
        pltpu.with_memory_space_constraint(came_pooled[0], pltpu.VMEM),
        *in_hbm([coarse]),
    )
    return (refined, coarse.reshape(slots * 8, pool_width))


def solution(mesh):
    placed = (
        P(("groups", "seq"), "mp"),
        P(),
        P(),
        P(),
        P(),
        P(),
        P(),
        P(),
        P(("groups", "seq", "mp")),
    )
    return jax.shard_map(
        body,
        mesh=mesh,
        in_specs=placed,
        out_specs=(P(("groups", "seq", "mp"), None), P(("groups", "seq", "mp"), None)),
        check_vma=False,
    )
```
